32 devices in a mesh: band: 2 (over core), grid: 16 (over z, y, x).
Axes of the slice: x: 2, y: 2, z: 4, core: 2. Of those that a mesh axis runs over, the one named last changes fastest.
Arguments:
- coefficients: float32 [4, 2, 128, 128, 128], P('band', None, 'grid'), may hold values from -0.01171875 to 0.01171875
- potential: float32 [128, 128, 128], P('grid'), may hold values from -3 to 3
- external: float32 [128, 128, 128], P('grid'), may hold values from -6 to 6
- core_density: float32 [128, 128, 128], P('grid'), may hold values from 0.05 to 0.5
- rotations: float32 [2, 4, 2], P(None, 'band'), may hold values from -2 to 3
- mlp_in: float32 [3, 32], replicated, may hold values from -4 to 4
- mlp_out: float32 [32], replicated, may hold values from -0.4 to 0.4
Outputs:
- new_coefficients: float32 [4, 2, 128, 128, 128], P('band', None, 'grid')
- new_potential: float32 [128, 128, 128], P('grid')
The draws below stay inside these ranges and needn't reach their ends.
All inputs are finite; a program needn't handle non-finite values.
Results may differ from the reference program's by a relative error of at most 0.0003.
Values sent between devices are 32-bit elements; how exact they have to be, the bound alone decides.
A program may use at most 64 MiB of HBM per device.

```python
import math
import jax
import jax.numpy as jnp
from jax import lax

NX = 128
NY = 128
NZ = 128
BLOC = 2
ITERS = 2
NH = 32
BANDS = 4
N_BAND = 2


def draw_rotations(key, part):
    jitter = jax.random.truncated_normal(key, -3.0, 3.0, (ITERS, BANDS, BLOC), jnp.float32)
    band_rows = lax.iota(jnp.int32, BANDS) % BLOC
    diagonal = (band_rows[:, None] == lax.iota(jnp.int32, BLOC)[None, :]).astype(jnp.float32)
    return diagonal[None] + 0.5 * jitter / math.sqrt(BLOC)


def block_scale(key, extent, pieces, low, high):
    gain = 1.0
    for position, shards_of in pieces:
        steps = jax.random.uniform(jax.random.fold_in(jax.random.fold_in(key, 6), position), (shards_of,), jnp.float32, low / len(pieces), high / len(pieces))
        gain = gain * jnp.repeat(jnp.exp(steps), extent[position] // shards_of).reshape((-1,) + (1,) * (len(extent) - 1 - position))
    return gain


def gaussian(stream_key, dims, scale, reach, pieces=(), kind=jnp.bfloat16):
    loudness = block_scale(stream_key, dims, pieces, -0.22, 0.18) if pieces else 1.0
    result = jax.random.normal(stream_key, dims, jnp.float32) * scale * loudness
    return jnp.minimum(jnp.maximum(result, -reach), reach).astype(kind)


def setup_inputs(seed: int = 0) -> dict:
    splits = jax.random.split(jax.random.key(seed), 8)
    coefficients = gaussian(splits[0], (BANDS, 2, NX, NY, NZ), (NX * NY * NZ // 8) ** -0.5, 0.01171875, ((0, 2), (2, 16)), jnp.float32)
    potential = gaussian(splits[1], (NY, NX, NZ), 0.5, 3.0, ((0, 16),), jnp.float32)
    external = gaussian(splits[2], (NY, NX, NZ), 1.0, 6.0, ((0, 16),), jnp.float32)
    core_density = jnp.clip(jnp.exp(math.log(0.5) - 2.3025851 * jax.random.uniform(splits[3], (NY, NX, NZ), jnp.float32) ** block_scale(splits[3], (NY, NX, NZ), ((0, 16),), -0.2, 0.2)), 0.05, 0.5)
    rotations = draw_rotations(jax.random.fold_in(splits[7], 71), 0)
    mlp_in = gaussian(splits[5], (3, NH), 1.0, 4.0, (), jnp.float32)
    mlp_out = gaussian(splits[6], (NH,), 0.1, 0.4, (), jnp.float32)
    return dict(coefficients=coefficients, potential=potential, external=external, core_density=core_density, rotations=rotations, mlp_in=mlp_in, mlp_out=mlp_out)


step_size = 0.2
epsilon = 1e-06
spacing = 0.58
kinetic_scale = 0.5 * (2.0 * math.pi / spacing) ** 2
coulomb_scale = spacing * spacing / math.pi
gradient_scale = 2.0 * math.pi / spacing
reduced_scale = 2.0 * (3.0 * math.pi * math.pi) ** (1.0 / 3.0)
exchange_scale = (3.0 / math.pi) ** (1.0 / 3.0)

def frequencies(points, offset, length):
    places = offset + lax.iota(jnp.int32, length)
    return jnp.where(2 * places < points, places, places - points)

def without_nyquist(values, points):
    return jnp.where(2 * values == -points, 0, values)

def reciprocal_tables(offset, length):
    along_x = frequencies(NX, offset, length)
    along_y = frequencies(NY, 0, NY)
    raw_z = frequencies(NZ, 0, NZ)
    along_z = raw_z * (NX // NZ)
    squared = along_x[:, None, None] * along_x[:, None, None] + along_y[None, :, None] * along_y[None, :, None] + along_z[None, None, :] * along_z[None, None, :]
    cutoff = (16 * squared <= NX * NX).astype(jnp.float32)
    kinetic = kinetic_scale * squared.astype(jnp.float32) / (NX * NX)
    coulomb = jnp.where(squared > 0, coulomb_scale * (NX * NX) / jnp.maximum(squared, 1).astype(jnp.float32), 0.0).astype(jnp.float32)
    slope_x = gradient_scale * without_nyquist(along_x, NX).astype(jnp.float32) / NX
    slope_y = gradient_scale * without_nyquist(along_y, NY).astype(jnp.float32) / NX
    slope_z = gradient_scale * (without_nyquist(raw_z, NZ) * (NX // NZ)).astype(jnp.float32) / NX
    return (cutoff, kinetic, coulomb, slope_x[:, None, None], slope_y[None, :, None], slope_z[None, None, :])

def toward_position_grid(spectral_amplitude):
    wave = spectral_amplitude[:, 0] + 1j * spectral_amplitude[:, 1]
    position_grid_values = jnp.fft.ifftn(wave, axes=(1, 2, 3)) * (NX * NY * NZ)
    position_grid_values = jnp.transpose(position_grid_values, (0, 2, 1, 3))
    return jnp.stack([position_grid_values.real, position_grid_values.imag], 1)

def toward_spectral_amplitudes(position_grid_values):
    wave = position_grid_values[:, 0] + 1j * position_grid_values[:, 1]
    wave = jnp.transpose(wave, (0, 2, 1, 3))
    spectral_amplitude = jnp.fft.fftn(wave, axes=(1, 2, 3)) / (NX * NY * NZ)
    return jnp.stack([spectral_amplitude.real, spectral_amplitude.imag], 1)

def refine_group(spectral_amplitude, rotation, potential, cutoff, kinetic):
    highest = lax.Precision.HIGHEST
    current = cutoff * spectral_amplitude
    for iteration in range(ITERS):
        applied = cutoff * (kinetic * current + toward_spectral_amplitudes(toward_position_grid(current) * potential))
        intersection = lax.optimization_barrier(jnp.sum(current * current, axis=(1, 2, 3, 4)))
        energy = lax.optimization_barrier(jnp.sum(current * applied, axis=(1, 2, 3, 4)))
        factor = 1.0 + step_size * (energy / (intersection + epsilon))
        updated = factor[:, None, None, None, None] * current - step_size * applied
        updated = jnp.einsum('ij,jcxyz->icxyz', rotation[iteration], updated, precision=highest)
        length = lax.optimization_barrier(jnp.sum(updated * updated, axis=(1, 2, 3, 4)))
        current = updated / jnp.sqrt(length + epsilon)[:, None, None, None, None]
    real_space = toward_position_grid(current)
    partial_value = 2.0 / BANDS * lax.optimization_barrier(jnp.sum(real_space * real_space, axis=(0, 1)))
    return (current, partial_value)

def reference(coefficients, potential, external, core_density, rotations, mlp_in, mlp_out):
    highest = lax.Precision.HIGHEST
    cutoff, kinetic, coulomb, slope_x, slope_y, slope_z = reciprocal_tables(0, NX)
    groups = coefficients.reshape(N_BAND, BLOC, 2, NX, NY, NZ)
    turns = jnp.transpose(rotations.reshape(ITERS, N_BAND, BLOC, BLOC), (1, 0, 2, 3))

    def one_group(group_pair):
        return refine_group(group_pair[0], group_pair[1], potential, cutoff, kinetic)
    refined, partials = lax.map(one_group, (groups, turns))
    density = lax.optimization_barrier(jnp.sum(partials, axis=0)) + core_density
    spectrum = toward_spectral_amplitudes(jnp.stack([density, jnp.zeros_like(density)])[None])[0]
    spec_real = spectrum[0]
    spec_imag = spectrum[1]
    first_real = coulomb * spec_real - slope_x * spec_real
    first_imag = coulomb * spec_imag - slope_x * spec_imag
    second_real = -slope_y * spec_imag - slope_z * spec_real
    second_imag = slope_y * spec_real - slope_z * spec_imag
    fields = toward_position_grid(jnp.stack([jnp.stack([first_real, first_imag]), jnp.stack([second_real, second_imag])]))
    hartree = fields[0, 0]
    change_x = fields[0, 1]
    change_y = fields[1, 0]
    change_z = fields[1, 1]
    cube_root = jnp.cbrt(density)
    gradient = jnp.sqrt(change_x * change_x + change_y * change_y + change_z * change_z)
    reduced = gradient / (reduced_scale * density * cube_root)
    bounded = reduced / (1.0 + reduced)
    hidden = jnp.tanh(mlp_in[0][:, None, None, None] * cube_root + mlp_in[1][:, None, None, None] * bounded + mlp_in[2][:, None, None, None])
    enhance = 1.0 + jnp.einsum('k,kyxz->yxz', mlp_out, hidden, precision=highest)
    new_potential = external + hartree - exchange_scale * cube_root * enhance
    return (refined.reshape(BANDS, 2, NX, NY, NZ), new_potential)
```

```python
import functools
import math

import jax
import jax.numpy as jnp
import numpy as np
from jax import lax
from jax.experimental import pallas as pl
from jax.experimental.pallas import tpu as pltpu
from jax.sharding import PartitionSpec as P

MESH = pl.DeviceIdType.MESH
F32 = jnp.float32
BF16 = jnp.bfloat16

step_size = 0.2
epsilon = 1e-06
spacing = 0.58
kinetic_scale = 0.5 * (2.0 * math.pi / spacing) ** 2
coulomb_scale = spacing * spacing / math.pi
gradient_scale = 2.0 * math.pi / spacing
reduced_scale = 2.0 * (3.0 * math.pi * math.pi) ** (1.0 / 3.0)
exchange_scale = (3.0 / math.pi) ** (1.0 / 3.0)


def halves(table):
    table = np.asarray(table, np.float32)
    high = table.astype(BF16)
    low = (table - high.astype(np.float32)).astype(BF16)
    return np.stack([high, low])


def split(value):
    high = value.astype(BF16)
    return high, (value - high.astype(F32)).astype(BF16)


def dot(a, b):
    return jnp.dot(a, b, preferred_element_type=F32)


def table_left(table, value):
    high, low = split(value)
    return dot(table[0], high) + (dot(table[0], low) + dot(table[1], high))


def table_right(value, table):
    high, low = split(value)
    return dot(high, table[0]) + (dot(low, table[0]) + dot(high, table[1]))


def band_tables(n, bands, points):
    half = points // 2
    slots = half // n
    keep = np.arange(half)
    keep = np.where(keep < half // 2, keep, keep - half)
    cell = np.arange(points)
    angle = 2.0 * np.pi * ((keep[:, None] * cell[None, :]) % points) / points
    cos, sin = np.cos(angle), np.sin(angle)
    top = 2.0 * np.pi * ((half // 2 * cell) % points) / points
    ctop, stop = np.cos(top), np.sin(top)
    y_out = np.concatenate([cos.T, sin.T], 1)
    y_in = np.concatenate([cos, sin], 1)
    z_out = np.block([[cos, sin], [-sin, cos]])
    z_in = np.block([[cos.T, -sin.T], [sin.T, cos.T]])
    rows = bands * half
    x_cos = np.zeros((bands, points, n, bands, slots))
    x_sin = np.zeros_like(x_cos)
    for b in range(bands):
        x_cos[b, :, :, b] = cos.T.reshape(points, n, slots)
        x_sin[b, :, :, b] = sin.T.reshape(points, n, slots)
    x_cos = x_cos.reshape(bands * points, rows)
    x_sin = x_sin.reshape(bands * points, rows)
    x_out = np.concatenate([x_cos, x_sin], 1)
    extra = np.zeros((2, 8, bands * points))
    for b in range(bands):
        extra[0, b, b * points : (b + 1) * points] = ctop
        extra[1, b, b * points : (b + 1) * points] = stop
    x_in = np.stack([np.concatenate([x_cos.T, extra[0]]), np.concatenate([x_sin.T, extra[1]])])
    ones, zeros = np.ones(points), np.zeros(points)
    point_out = np.zeros((3, points, 2 * points))
    point_in = np.zeros((3, 2 * points, points))
    for i, (c, s) in enumerate(((ones, zeros), (ctop, stop), (ones, zeros))):
        point_out[i, i + 1] = np.concatenate([c, s])
        point_out[i, half + i + 1] = np.concatenate([-s, c])
        point_in[i, :, i + 1] = np.concatenate([c, s])
        point_in[i, :, half + i + 1] = np.concatenate([-s, c])
    return [halves(t) for t in (y_out, y_in, z_out, z_in, x_out, x_in[0], x_in[1])] + [
        np.moveaxis(halves(point_out), 1, 0),
        np.moveaxis(halves(point_in), 1, 0),
        np.stack([ctop, stop]).astype(np.float32)[:, :, None],
    ]


def band_kernel(
    n, peers, bands, points, iters,
    packed, special, mask, kinetic, potential, core, rotations,
    y_out, y_in, z_out, z_in, x_out, x_in_c, x_in_s, point_out, point_in, phase, y_phase,
    new_out, special_out, density_out,
    current, applied, sent, got, grams, grams_got, levels_r, levels_i, mixed,
    special_got, part, part_got, send_sem, recv_sem, gram_send, gram_recv, first_sem, last_sem, dens_sem,
):
    me = lax.axis_index("grid")
    band = lax.axis_index("band")
    half = points // 2
    slots = half // n
    planes = points // n
    rows = bands * half
    home = n // 2
    high_owner = (half // 2) // planes

    def at(grid):
        return {"band": band, "grid": grid}

    barrier = pltpu.get_barrier_semaphore()

    @pl.loop(1, n)
    def _(i):
        pl.semaphore_signal(barrier, inc=1, device_id=at(lax.rem(me + i, n)), device_id_type=MESH)

    for i in range(1, peers):
        pl.semaphore_signal(
            barrier, inc=1, device_id={"band": lax.rem(band + i, peers), "grid": me}, device_id_type=MESH
        )
    pl.semaphore_wait(barrier, n - 1 + peers - 1)

    def plane_of(device):
        slot = device * slots
        return jnp.where(slot < half // 2, slot, slot + half)

    def first_copy(target):
        start = plane_of(target)
        return pltpu.make_async_remote_copy(
            src_ref=packed.at[:, pl.ds(lax.rem(start, planes), slots)],
            dst_ref=current,
            send_sem=first_sem.at[5 + lax.rem(start, planes) // slots],
            recv_sem=first_sem.at[1],
            device_id=at(target),
            device_id_type=MESH,
        )

    def first_own():
        return pltpu.make_async_copy(
            packed.at[:, pl.ds(lax.rem(plane_of(me), planes), slots)], current, first_sem.at[1]
        )

    def point_copy(place):
        return pltpu.make_async_remote_copy(
            src_ref=special,
            dst_ref=special_got.at[place],
            send_sem=first_sem.at[place * 2],
            recv_sem=first_sem.at[3 + place],
            device_id=at(home),
            device_id_type=MESH,
        )

    source = plane_of(me) // planes

    @pl.when(source == me)
    def _():
        first_own().start()

    @pl.loop(0, n)
    def _(target):
        @pl.when(jnp.logical_and(plane_of(target) // planes == me, target != me))
        def _():
            first_copy(target).start()

    @pl.when(me == 0)
    def _():
        point_copy(0).start()

    @pl.when(me == high_owner)
    def _():
        point_copy(1).start()

    @pl.loop(0, n)
    def _(target):
        @pl.when(jnp.logical_and(plane_of(target) // planes == me, target != me))
        def _():
            first_copy(target).wait_send()

    @pl.when(me == 0)
    def _():
        point_copy(0).wait_send()

    @pl.when(me == high_owner)
    def _():
        point_copy(1).wait_send()

    @pl.when(source == me)
    def _():
        first_own().wait()

    @pl.when(source != me)
    def _():
        first_copy(me).wait_recv()

    @pl.when(me == home)
    def _():
        point_copy(0).wait_recv()
        point_copy(1).wait_recv()
        for b in range(bands):
            current[b, 0, 0:8, :] = current[b, 0, 0:8, :] * mask[0, 0:8, :] * special[0, 8:16, :] + (
                special_got[0, b, 0:8, :] + special_got[1, b, 0:8, :]
            )

    for b in range(bands):
        current[b] = current[b] * mask[...]

    lanes = lax.broadcasted_iota(jnp.int32, (1, points), 1)
    sign = jnp.where(lanes < half, -1.0, 1.0).astype(F32)
    alone = jnp.where(lax.rem(lanes, half) == 0, 1.0, 0.0).astype(F32)

    def turn(value):
        return pltpu.roll(value, half, 1) * sign

    def exchange(stage, with_gram):
        def copies(target, origin):
            found = [
                pltpu.make_async_remote_copy(
                    src_ref=sent.at[stage, target],
                    dst_ref=got.at[stage, origin],
                    send_sem=send_sem.at[stage, target],
                    recv_sem=recv_sem.at[stage, origin],
                    device_id=at(target),
                    device_id_type=MESH,
                )
            ]
            if with_gram is not None:
                found.append(
                    pltpu.make_async_remote_copy(
                        src_ref=grams.at[with_gram],
                        dst_ref=grams_got.at[with_gram, origin],
                        send_sem=gram_send.at[with_gram, target],
                        recv_sem=gram_recv.at[with_gram, origin],
                        device_id=at(target),
                        device_id_type=MESH,
                    )
                )
            return found

        @pl.loop(1, n)
        def _(i):
            for copy in copies(lax.rem(me + i, n), me):
                copy.start()

        own = pltpu.make_async_copy(sent.at[stage, me], got.at[stage, me], recv_sem.at[stage, me])
        own.start()
        if with_gram is not None:
            mine = pltpu.make_async_copy(
                grams.at[with_gram], grams_got.at[with_gram, me], gram_recv.at[with_gram, me]
            )
            mine.start()
            mine.wait()
        own.wait()

        @pl.loop(1, n)
        def _(i):
            for copy in copies(lax.rem(me + i, n), me):
                copy.wait_send()
            origin = lax.rem(me + n - i, n)
            for copy in copies(origin, origin):
                copy.wait_recv()

    def y_outward(source_ref, stage):
        for b in range(bands):
            for x in range(slots):
                value = source_ref[b, x]
                full = table_left(y_out, jnp.concatenate([value, turn(value)], 0))
                sent[stage, :, b, x] = full.reshape(n, planes, points)

    def y_inward(stage, b, x):
        value = got[stage, :, b, x].reshape(points, points)
        return table_left(y_in, jnp.concatenate([value, -turn(value)], 0))

    def swapped(value, s):
        return jnp.concatenate([s * value[:, points:], -s * value[:, :points]], 1)

    y_phase_c = y_phase[0]
    y_phase_s = y_phase[1]

    def space(y_action):
        points_x, points_row = [], []
        for b in range(bands):
            row = mixed[home, b, 0]
            points_x.append(table_right(row, point_out[0]))
            along_z = table_right(row, point_out[1])
            along_y = table_right(row, point_out[2])
            points_row.append(along_z + along_y * y_phase_c + swapped(along_y, -1.0) * y_phase_s)
            mixed[home, b, 0] = row * alone
        levels = table_right(mixed[...].reshape(rows * planes, points), z_out)
        levels_r[0 : rows * planes, :] = levels[:, :points]
        levels_i[0 : rows * planes, :] = levels[:, points:]
        for y in range(planes):
            real = levels_r[pl.ds(y, rows, stride=planes), :]
            imag = levels_i[pl.ds(y, rows, stride=planes), :]
            stacked = jnp.concatenate(
                [jnp.concatenate([real, imag], 1), jnp.concatenate([-imag, real], 1)], 0
            )
            wave = table_left(x_out, stacked)
            found = []
            for b in range(bands):
                at_x = points_x[b][y : y + 1]
                found.append(
                    wave[b * points : (b + 1) * points]
                    + phase[0] * at_x
                    + phase[1] * swapped(at_x, -1.0)
                    + points_row[b][y : y + 1]
                )
            y_action(y, found)

    def spectrum(stage):
        def action(y, found):
            field = potential[y]
            product = jnp.concatenate([f * jnp.concatenate([field, field], 1) for f in found], 0)
            slotted = table_left(x_in_c, product) + table_left(x_in_s, swapped(product, 1.0))
            levels_r[pl.ds(y, rows + 8, stride=planes), :] = slotted[:, :points]
            levels_i[pl.ds(y, rows + 8, stride=planes), :] = slotted[:, points:]

        space(action)
        both = jnp.concatenate([levels_r[...], levels_i[...]], 1)
        found = table_right(both[0 : rows * planes], z_in).reshape(n, bands, slots, planes, points)
        sent[stage] = found
        for b in range(bands):
            start = (rows + b) * planes
            top = both[start : start + planes]
            zero = both[b * slots * planes : b * slots * planes + planes]
            last = table_right(zero, point_in[2])
            last = last * y_phase_c - turn(last) * y_phase_s
            sent[stage, home, b, 0] = (
                sent[stage, home, b, 0] * alone
                + table_right(top, point_in[0])
                + table_right(zero, point_in[1])
                + last
            )

    def pairs():
        return [(i, j) for i in range(bands) for j in range(bands)]

    def mixing(which, turn_at):
        total = jnp.sum(jnp.sum(grams_got[which], 0), 1, keepdims=True)
        square = bands * bands
        cc = {ij: total[k : k + 1] for k, ij in enumerate(pairs())}
        ca = {ij: total[square + k : square + k + 1] for k, ij in enumerate(pairs())}
        aa = {ij: total[2 * square + k : 2 * square + k + 1] for k, ij in enumerate(pairs())}
        factor = [1.0 + step_size * (ca[i, i] / (cc[i, i] + epsilon)) for i in range(bands)]
        moved = {
            (i, j): factor[i] * factor[j] * cc[i, j]
            - step_size * (factor[i] * ca[i, j] + factor[j] * ca[j, i])
            + step_size * step_size * aa[i, j]
            for i, j in pairs()
        }
        weights = []
        for b in range(bands):
            r = [rotations[turn_at, b, c] for c in range(bands)]
            length = sum(r[i] * r[j] * moved[i, j] for i, j in pairs())
            scale = lax.rsqrt(jnp.maximum(length, 0.0) + epsilon)
            weights.append([(scale * r[c] * factor[c], scale * r[c] * (-step_size)) for c in range(bands)])
        return weights

    y_outward(current, 0)
    exchange(0, None)
    mixed[...] = got[0]
    stage = 0
    for t in range(iters):
        spectrum(stage + 1)
        exchange(stage + 1, None)
        for b in range(bands):
            for x in range(slots):
                applied[b, x] = mask[x] * (
                    kinetic[x] * current[b, x] + y_inward(stage + 1, b, x) * (1.0 / points**3)
                )
        for k, (i, j) in enumerate(pairs()):
            for q, (u, v) in enumerate(((current, current), (current, applied), (applied, applied))):
                product = jnp.sum((u[i] * v[j]).reshape(slots * half, points), 0, keepdims=True)
                grams[t, q * bands * bands + k : q * bands * bands + k + 1, :] = product
        y_outward(applied, stage + 2)
        exchange(stage + 2, t)
        weights = mixing(t, t)
        old = [got[0, :, b] for b in range(bands)]
        new_mixed, new_current = [], []
        for b in range(bands):
            new_mixed.append(
                sum(weights[b][c][0] * old[c] + weights[b][c][1] * got[stage + 2, :, c] for c in range(bands))
            )
            new_current.append(
                sum(weights[b][c][0] * current[c] + weights[b][c][1] * applied[c] for c in range(bands))
            )
        for b in range(bands):
            current[b] = new_current[b]
            mixed[:, b] = new_mixed[b]
            got[0, :, b] = new_mixed[b]
        stage += 2

    def last_arrival(origin):
        place = new_out.at[:, pl.ds(lax.rem(plane_of(origin), planes), slots)]
        return pltpu.make_async_remote_copy(
            src_ref=current,
            dst_ref=place,
            send_sem=last_sem.at[0],
            recv_sem=last_sem.at[4 + lax.rem(plane_of(origin), planes) // slots],
            device_id=at(origin),
            device_id_type=MESH,
        )

    def last_sent():
        return pltpu.make_async_remote_copy(
            src_ref=current,
            dst_ref=new_out.at[:, pl.ds(lax.rem(plane_of(me), planes), slots)],
            send_sem=last_sem.at[0],
            recv_sem=last_sem.at[4 + lax.rem(plane_of(me), planes) // slots],
            device_id=at(source),
            device_id_type=MESH,
        )

    def last_own():
        return pltpu.make_async_copy(
            current, new_out.at[:, pl.ds(lax.rem(plane_of(me), planes), slots)], last_sem.at[0]
        )

    def point_back(target, sem):
        return pltpu.make_async_remote_copy(
            src_ref=current.at[:, 0, pl.ds(0, 8)],
            dst_ref=special_out,
            send_sem=last_sem.at[sem],
            recv_sem=last_sem.at[3],
            device_id=at(target),
            device_id_type=MESH,
        )

    @pl.when(source == me)
    def _():
        last_own().start()

    @pl.when(source != me)
    def _():
        last_sent().start()

    @pl.when(me == home)
    def _():
        point_back(0, 1).start()
        point_back(high_owner, 2).start()

    @pl.when(jnp.logical_and(me != 0, me != high_owner))
    def _():
        special_out[...] = jnp.zeros_like(special_out)

    @pl.when(jnp.logical_and(me * planes >= half // 2, me * planes < points - half // 2))
    def _():
        new_out[...] = jnp.zeros_like(new_out)

    def density(y, found):
        total = sum(f[:, :points] * f[:, :points] + f[:, points:] * f[:, points:] for f in found)
        part[y] = total * (2.0 / (bands * peers))

    space(density)

    def swap(i):
        return pltpu.make_async_remote_copy(
            src_ref=part,
            dst_ref=part_got.at[i - 1],
            send_sem=dens_sem.at[0, i - 1],
            recv_sem=dens_sem.at[1, i - 1],
            device_id={"band": lax.rem(band + i, peers), "grid": me},
            device_id_type=MESH,
        )

    for i in range(1, peers):
        swap(i).start()
    for i in range(1, peers):
        swap(i).wait()
    total = part[...] + core[...]
    for i in range(1, peers):
        total = total + part_got[i - 1]
    density_out[...] = total

    @pl.when(source == me)
    def _():
        last_own().wait()

    @pl.when(source != me)
    def _():
        last_sent().wait_send()

    @pl.when(me == home)
    def _():
        point_back(0, 1).wait_send()
        point_back(high_owner, 2).wait_send()

    @pl.when(jnp.logical_or(me == 0, me == high_owner))
    def _():
        point_back(home, 1).wait_recv()

    @pl.loop(0, n)
    def _(origin):
        @pl.when(jnp.logical_and(plane_of(origin) // planes == me, origin != me))
        def _():
            last_arrival(origin).wait_recv()


def update_bands(coefficients, potential, core, rotations):
    n, peers = lax.axis_size("grid"), lax.axis_size("band")
    bands, _, planes, points, _ = coefficients.shape
    iters = rotations.shape[0]
    half, quarter = points // 2, points // 4
    slots = half // n
    me = lax.axis_index("grid")

    def keep(value, axis):
        low = lax.slice_in_dim(value, 0, quarter, axis=axis)
        high = lax.slice_in_dim(value, points - quarter, points, axis=axis)
        return jnp.concatenate([low, high], axis)

    kept = keep(keep(coefficients, 3), 4)
    packed = jnp.concatenate([kept[:, 0], kept[:, 1]], -1)
    along_x = jnp.where(me == quarter // planes, coefficients[:, :, quarter % planes, 0, 0], 0.0)
    along_z = jnp.where(me == 0, coefficients[:, :, 0, 0, quarter], 0.0)
    along_y = jnp.where(me == 0, coefficients[:, :, 0, quarter, 0], 0.0)
    row = jnp.stack([jnp.zeros_like(along_x), along_x, along_z, along_y], -1)
    row = jnp.pad(row, ((0, 0), (0, 0), (0, half - 4))).reshape(bands, 1, points)
    lane = lax.iota(jnp.int32, points)
    zero_lane = (lane % half == 0).astype(F32)
    special = jnp.concatenate(
        [jnp.pad(row, ((0, 0), (0, 7), (0, 0))), jnp.broadcast_to(zero_lane, (bands, 8, points))], 1
    )

    def frequency(slot):
        return jnp.where(slot < quarter, slot, slot - half)

    gx = frequency(me * slots + lax.iota(jnp.int32, slots))[:, None, None]
    gy = frequency(lax.iota(jnp.int32, half))[None, :, None]
    gz = frequency(lane % half)[None, None, :]
    squared = gx * gx + gy * gy + gz * gz
    spot = (gx == -quarter) & (gy == 0) & (lane % half < 4)[None, None, :]
    squared = jnp.where(spot, quarter * quarter, squared)
    mask = (16 * squared <= points * points).astype(F32)
    kinetic = kinetic_scale * squared.astype(F32) / (points * points)

    rows = bands * half
    vmem = pl.BlockSpec(memory_space=pltpu.VMEM)
    smem = pl.BlockSpec(memory_space=pltpu.SMEM)
    stages = 2 * iters + 1
    chunk = (bands, slots, planes, points)
    gram_rows = -(-3 * bands * bands // 8) * 8
    dma = pltpu.SemaphoreType.DMA
    tables = band_tables(n, bands, points)
    y_phase = lax.dynamic_slice_in_dim(jnp.asarray(tables[-1]), me * planes, planes, 1)
    new, back, density = pl.pallas_call(
        functools.partial(band_kernel, n, peers, bands, points, iters),
        out_shape=(
            jax.ShapeDtypeStruct((bands, planes, half, points), F32),
            jax.ShapeDtypeStruct((bands, 8, points), F32),
            jax.ShapeDtypeStruct((planes, points, points), F32),
        ),
        in_specs=[vmem] * 6 + [smem] + [vmem] * (len(tables) + 1),
        out_specs=(vmem, vmem, vmem),
        scratch_shapes=[
            pltpu.VMEM((bands, slots, half, points), F32),
            pltpu.VMEM((bands, slots, half, points), F32),
            pltpu.VMEM((stages, n) + chunk, F32),
            pltpu.VMEM((stages, n) + chunk, F32),
            pltpu.VMEM((iters, gram_rows, points), F32),
            pltpu.VMEM((iters, n, gram_rows, points), F32),
            pltpu.VMEM(((rows + 8) * planes, points), F32),
            pltpu.VMEM(((rows + 8) * planes, points), F32),
            pltpu.VMEM((n,) + chunk, F32),
            pltpu.VMEM((2, bands, 16, points), F32),
            pltpu.VMEM((planes, points, points), F32),
            pltpu.VMEM((max(peers - 1, 1), planes, points, points), F32),
            dma((stages, n)),
            dma((stages, n)),
            dma((iters, n)),
            dma((iters, n)),
            dma((5 + planes // slots,)),
            dma((4 + planes // slots,)),
            dma((2, max(peers - 1, 1))),
        ],
        compiler_params=pltpu.CompilerParams(
            collective_id=0, has_side_effects=True, vmem_limit_bytes=60 * 2**20
        ),
    )(packed, special, mask, kinetic, potential, core, rotations, *tables, y_phase)

    parts = jnp.stack([new[..., :half], new[..., half:]], 1)

    def widen(value, axis):
        low = lax.slice_in_dim(value, 0, quarter, axis=axis)
        high = lax.slice_in_dim(value, quarter, half, axis=axis)
        shape = list(value.shape)
        shape[axis] = points - half
        return jnp.concatenate([low, jnp.zeros(shape, F32), high], axis)

    gx_own = me * planes + lax.iota(jnp.int32, planes)
    live = (gx_own != points - quarter)[:, None, None] | (
        (lax.iota(jnp.int32, half) == 0)[None, :, None] & (lax.iota(jnp.int32, half) == 0)[None, None, :]
    )
    kept_plane = ((gx_own < quarter) | (gx_own >= points - quarter))[:, None, None]
    wide = widen(widen(jnp.where(live & kept_plane, parts, 0.0), 3), 4)
    found = back[:, 0].reshape(bands, 2, half)
    i_x = lax.broadcasted_iota(jnp.int32, (1, 1, planes, points, points), 2) + me * planes
    i_y = lax.broadcasted_iota(jnp.int32, (1, 1, planes, points, points), 3)
    i_z = lax.broadcasted_iota(jnp.int32, (1, 1, planes, points, points), 4)

    def spread(k):
        return found[:, :, k][:, :, None, None, None]

    wide = jnp.where((i_x == quarter) & (i_y == 0) & (i_z == 0), spread(1), wide)
    wide = jnp.where((i_x == 0) & (i_y == 0) & (i_z == quarter), spread(2), wide)
    wide = jnp.where((i_x == 0) & (i_y == quarter) & (i_z == 0), spread(3), wide)
    return wide, density


def frequencies(points, offset, length):
    places = offset + lax.iota(jnp.int32, length)
    return jnp.where(2 * places < points, places, places - points)


def without_nyquist(values, points):
    return jnp.where(2 * values == -points, 0, values)


def reciprocal_tables(points, offset, length):
    along_x = frequencies(points, offset, length)
    along = frequencies(points, 0, points)
    squared = (
        along_x[:, None, None] * along_x[:, None, None]
        + along[None, :, None] * along[None, :, None]
        + along[None, None, :] * along[None, None, :]
    )
    return jnp.where(
        squared > 0, coulomb_scale * (points * points) / jnp.maximum(squared, 1).astype(F32), 0.0
    )


def body(coefficients, potential, external, core_density, rotations, mlp_in, mlp_out):
    highest = lax.Precision.HIGHEST
    points = potential.shape[1]
    planes = coefficients.shape[2]
    offset = lax.axis_index("grid") * planes
    current, density = update_bands(coefficients, potential, core_density, rotations)

    coulomb = reciprocal_tables(points, offset, planes)
    cell = np.arange(points)
    angle = 2.0 * np.pi * ((cell[:, None] * cell[None, :]) % points) / points
    cos, sin = np.cos(angle), np.sin(angle)
    freq = np.where(2 * cell < points, cell, cell - points)
    slope = gradient_scale * np.where(2 * freq == -points, 0, freq) / points
    back = (np.exp(1j * angle) * slope[None, :] * 1j) @ np.exp(-1j * angle) / points
    slope_table = np.ascontiguousarray(back.real).astype(np.float32)
    cos32, sin32 = cos.astype(np.float32), sin.astype(np.float32)

    def mm(pattern, a, b):
        return jnp.einsum(pattern, a, b, precision=highest)

    varying = density - 2.275
    change_x = mm("yxz,ux->yuz", varying, slope_table)
    change_z = mm("yxz,wz->yxw", varying, slope_table)
    ar = mm("yxz,zw->yxw", varying, cos32)
    ai = mm("yxz,zw->yxw", varying, -sin32)
    br = mm("yxz,xu->yuz", ar, cos32) + mm("yxz,xu->yuz", ai, sin32)
    bi = mm("yxz,xu->yuz", ai, cos32) - mm("yxz,xu->yuz", ar, sin32)
    spec = jnp.stack([br, bi])
    spec = lax.all_to_all(spec, "grid", split_axis=2, concat_axis=1, tiled=True)
    sr, si = spec[0], spec[1]
    cr = mm("yxz,yv->xvz", sr, cos32) + mm("yxz,yv->xvz", si, sin32)
    ci = mm("yxz,yv->xvz", si, cos32) - mm("yxz,yv->xvz", sr, sin32)
    scale = coulomb * (1.0 / points**3)
    slope_y = jnp.asarray((slope / points**3).astype(np.float32))[None, :, None]
    fr = cr * scale - slope_y * cr
    fi = ci * scale - slope_y * ci
    gr = mm("xyz,yv->vxz", fr, cos32) - mm("xyz,yv->vxz", fi, sin32)
    gi = mm("xyz,yv->vxz", fi, cos32) + mm("xyz,yv->vxz", fr, sin32)
    spec = lax.all_to_all(jnp.stack([gr, gi]), "grid", split_axis=1, concat_axis=2, tiled=True)
    sr, si = spec[0], spec[1]
    hr = mm("yxz,xu->yuz", sr, cos32) - mm("yxz,xu->yuz", si, sin32)
    hi = mm("yxz,xu->yuz", si, cos32) + mm("yxz,xu->yuz", sr, sin32)
    hartree = mm("yxz,zw->yxw", hr, cos32) - mm("yxz,zw->yxw", hi, sin32)
    change_y = mm("yxz,zw->yxw", hi, cos32) + mm("yxz,zw->yxw", hr, sin32)

    cube_root = jnp.cbrt(density)
    gradient = jnp.sqrt(change_x * change_x + change_y * change_y + change_z * change_z)
    reduced = gradient / (reduced_scale * density * cube_root)
    bounded = reduced / (1.0 + reduced)
    enhance = jnp.ones_like(density)
    for k in range(mlp_out.shape[0]):
        enhance = enhance + mlp_out[k] * jnp.tanh(mlp_in[0, k] * cube_root + mlp_in[1, k] * bounded + mlp_in[2, k])
    new_potential = external + hartree - exchange_scale * cube_root * enhance
    return (current, new_potential)


def solution(mesh):
    in_specs = (
        P("band", None, "grid", None, None),
        P("grid", None, None),
        P("grid", None, None),
        P("grid", None, None),
        P(None, "band", None),
        P(),
        P(),
    )
    out_specs = (P("band", None, "grid", None, None), P("grid", None, None))
    return jax.shard_map(body, mesh=mesh, in_specs=in_specs, out_specs=out_specs, check_vma=False)
```

```python
import functools
import math

import jax
import jax.numpy as jnp
import numpy as np
from jax import lax
from jax.experimental import pallas as pl
from jax.experimental.pallas import tpu as pltpu
from jax.sharding import PartitionSpec as P

MESH = pl.DeviceIdType.MESH
F32 = jnp.float32
BF16 = jnp.bfloat16

step_size = 0.2
epsilon = 1e-06
spacing = 0.58
kinetic_scale = 0.5 * (2.0 * math.pi / spacing) ** 2
coulomb_scale = spacing * spacing / math.pi
gradient_scale = 2.0 * math.pi / spacing
reduced_scale = 2.0 * (3.0 * math.pi * math.pi) ** (1.0 / 3.0)
exchange_scale = (3.0 / math.pi) ** (1.0 / 3.0)


def halves(table):
    table = np.asarray(table, np.float32)
    high = table.astype(BF16)
    low = (table - high.astype(np.float32)).astype(BF16)
    return np.stack([high, low])


def split(value):
    high = value.astype(BF16)
    return high, (value - high.astype(F32)).astype(BF16)


def dot(a, b):
    return jnp.dot(a, b, preferred_element_type=F32)


def table_left(table, value):
    high, low = split(value)
    return dot(table[0], high) + (dot(table[0], low) + dot(table[1], high))


def table_right(value, table):
    high, low = split(value)
    return dot(high, table[0]) + (dot(low, table[0]) + dot(high, table[1]))


def band_tables(n, bands, points):
    half = points // 2
    slots = half // n
    keep = np.arange(half)
    keep = np.where(keep < half // 2, keep, keep - half)
    cell = np.arange(points)
    angle = 2.0 * np.pi * ((keep[:, None] * cell[None, :]) % points) / points
    cos, sin = np.cos(angle), np.sin(angle)
    top = 2.0 * np.pi * ((half // 2 * cell) % points) / points
    ctop, stop = np.cos(top), np.sin(top)
    y_out = np.concatenate([cos.T, sin.T], 1)
    y_in = np.concatenate([cos, sin], 1)
    z_out = np.block([[cos, sin], [-sin, cos]])
    z_in = np.block([[cos.T, -sin.T], [sin.T, cos.T]])
    rows = bands * half
    x_cos = np.zeros((bands, points, n, bands, slots))
    x_sin = np.zeros_like(x_cos)
    for b in range(bands):
        x_cos[b, :, :, b] = cos.T.reshape(points, n, slots)
        x_sin[b, :, :, b] = sin.T.reshape(points, n, slots)
    x_cos = x_cos.reshape(bands * points, rows)
    x_sin = x_sin.reshape(bands * points, rows)
    x_out = np.concatenate([x_cos, x_sin], 1)
    extra = np.zeros((2, 8, bands * points))
    for b in range(bands):
        extra[0, b, b * points : (b + 1) * points] = ctop
        extra[1, b, b * points : (b + 1) * points] = stop
    x_in = np.stack([np.concatenate([x_cos.T, extra[0]]), np.concatenate([x_sin.T, extra[1]])])
    ones, zeros = np.ones(points), np.zeros(points)
    point_out = np.zeros((3, points, 2 * points))
    point_in = np.zeros((3, 2 * points, points))
    for i, (c, s) in enumerate(((ones, zeros), (ctop, stop), (ones, zeros))):
        point_out[i, i + 1] = np.concatenate([c, s])
        point_out[i, half + i + 1] = np.concatenate([-s, c])
        point_in[i, :, i + 1] = np.concatenate([c, s])
        point_in[i, :, half + i + 1] = np.concatenate([-s, c])
    return [halves(t) for t in (y_out, y_in, z_out, z_in, x_out, x_in[0], x_in[1])] + [
        np.moveaxis(halves(point_out), 1, 0),
        np.moveaxis(halves(point_in), 1, 0),
        np.stack([ctop, stop]).astype(np.float32)[:, :, None],
    ]


def band_kernel(
    n, peers, bands, points, iters,
    packed, special, mask, kinetic, potential, core, rotations,
    y_out, y_in, z_out, z_in, x_out, x_in_c, x_in_s, point_out, point_in, phase, y_phase,
    new_out, special_out, density_out,
    current, applied, sent, got, grams, grams_got, levels_r, levels_i, mixed,
    special_got, part, part_got, send_sem, recv_sem, gram_send, gram_recv, first_sem, last_sem, dens_sem,
):
    me = lax.axis_index("grid")
    band = lax.axis_index("band")
    half = points // 2
    slots = half // n
    planes = points // n
    rows = bands * half
    home = n // 2
    high_owner = (half // 2) // planes

    def at(grid):
        return {"band": band, "grid": grid}

    barrier = pltpu.get_barrier_semaphore()

    @pl.loop(1, n)
    def _(i):
        pl.semaphore_signal(barrier, inc=1, device_id=at(lax.rem(me + i, n)), device_id_type=MESH)

    for i in range(1, peers):
        pl.semaphore_signal(
            barrier, inc=1, device_id={"band": lax.rem(band + i, peers), "grid": me}, device_id_type=MESH
        )
    pl.semaphore_wait(barrier, n - 1 + peers - 1)

    def plane_of(device):
        slot = device * slots
        return jnp.where(slot < half // 2, slot, slot + half)

    def first_copy(target):
        start = plane_of(target)
        return pltpu.make_async_remote_copy(
            src_ref=packed.at[:, pl.ds(lax.rem(start, planes), slots)],
            dst_ref=current,
            send_sem=first_sem.at[5 + lax.rem(start, planes) // slots],
            recv_sem=first_sem.at[1],
            device_id=at(target),
            device_id_type=MESH,
        )

    def first_own():
        return pltpu.make_async_copy(
            packed.at[:, pl.ds(lax.rem(plane_of(me), planes), slots)], current, first_sem.at[1]
        )

    def point_copy(place):
        return pltpu.make_async_remote_copy(
            src_ref=special,
            dst_ref=special_got.at[place],
            send_sem=first_sem.at[place * 2],
            recv_sem=first_sem.at[3 + place],
            device_id=at(home),
            device_id_type=MESH,
        )

    source = plane_of(me) // planes

    @pl.when(source == me)
    def _():
        first_own().start()

    @pl.loop(0, n)
    def _(target):
        @pl.when(jnp.logical_and(plane_of(target) // planes == me, target != me))
        def _():
            first_copy(target).start()

    @pl.when(me == 0)
    def _():
        point_copy(0).start()

    @pl.when(me == high_owner)
    def _():
        point_copy(1).start()

    @pl.loop(0, n)
    def _(target):
        @pl.when(jnp.logical_and(plane_of(target) // planes == me, target != me))
        def _():
            first_copy(target).wait_send()

    @pl.when(me == 0)
    def _():
        point_copy(0).wait_send()

    @pl.when(me == high_owner)
    def _():
        point_copy(1).wait_send()

    @pl.when(source == me)
    def _():
        first_own().wait()

    @pl.when(source != me)
    def _():
        first_copy(me).wait_recv()

    @pl.when(me == home)
    def _():
        point_copy(0).wait_recv()
        point_copy(1).wait_recv()
        for b in range(bands):
            current[b, 0, 0:8, :] = current[b, 0, 0:8, :] * mask[0, 0:8, :] * special[0, 8:16, :] + (
                special_got[0, b, 0:8, :] + special_got[1, b, 0:8, :]
            )

    for b in range(bands):
        current[b] = current[b] * mask[...]

    lanes = lax.broadcasted_iota(jnp.int32, (1, points), 1)
    sign = jnp.where(lanes < half, -1.0, 1.0).astype(F32)
    alone = jnp.where(lax.rem(lanes, half) == 0, 1.0, 0.0).astype(F32)

    def turn(value):
        return pltpu.roll(value, half, 1) * sign

    def exchange(stage, with_gram):
        def copies(target, origin):
            found = [
                pltpu.make_async_remote_copy(
                    src_ref=sent.at[stage, target],
                    dst_ref=got.at[stage, origin],
                    send_sem=send_sem.at[stage, target],
                    recv_sem=recv_sem.at[stage, origin],
                    device_id=at(target),
                    device_id_type=MESH,
                )
            ]
            if with_gram is not None:
                found.append(
                    pltpu.make_async_remote_copy(
                        src_ref=grams.at[with_gram],
                        dst_ref=grams_got.at[with_gram, origin],
                        send_sem=gram_send.at[with_gram, target],
                        recv_sem=gram_recv.at[with_gram, origin],
                        device_id=at(target),
                        device_id_type=MESH,
                    )
                )
            return found

        @pl.loop(1, n)
        def _(i):
            for copy in copies(lax.rem(me + i, n), me):
                copy.start()

        own = pltpu.make_async_copy(sent.at[stage, me], got.at[stage, me], recv_sem.at[stage, me])
        own.start()
        if with_gram is not None:
            mine = pltpu.make_async_copy(
                grams.at[with_gram], grams_got.at[with_gram, me], gram_recv.at[with_gram, me]
            )
            mine.start()
            mine.wait()
        own.wait()

        @pl.loop(1, n)
        def _(i):
            for copy in copies(lax.rem(me + i, n), me):
                copy.wait_send()
            origin = lax.rem(me + n - i, n)
            for copy in copies(origin, origin):
                copy.wait_recv()

    def y_outward(source_ref, stage):
        for b in range(bands):
            for x in range(slots):
                value = source_ref[b, x]
                full = table_left(y_out, jnp.concatenate([value, turn(value)], 0))
                sent[stage, :, b, x] = full.reshape(n, planes, points)

    def y_inward(stage, b, x):
        value = got[stage, :, b, x].reshape(points, points)
        return table_left(y_in, jnp.concatenate([value, -turn(value)], 0))

    def swapped(value, s):
        return jnp.concatenate([s * value[:, points:], -s * value[:, :points]], 1)

    y_phase_c = y_phase[0]
    y_phase_s = y_phase[1]

    def space(y_action):
        points_x, points_row = [], []
        for b in range(bands):
            row = mixed[home, b, 0]
            points_x.append(table_right(row, point_out[0]))
            along_z = table_right(row, point_out[1])
            along_y = table_right(row, point_out[2])
            points_row.append(along_z + along_y * y_phase_c + swapped(along_y, -1.0) * y_phase_s)
            mixed[home, b, 0] = row * alone
        levels = table_right(mixed[...].reshape(rows * planes, points), z_out)
        levels_r[0 : rows * planes, :] = levels[:, :points]
        levels_i[0 : rows * planes, :] = levels[:, points:]
        for y in range(planes):
            real = levels_r[pl.ds(y, rows, stride=planes), :]
            imag = levels_i[pl.ds(y, rows, stride=planes), :]
            stacked = jnp.concatenate(
                [jnp.concatenate([real, imag], 1), jnp.concatenate([-imag, real], 1)], 0
            )
            wave = table_left(x_out, stacked)
            found = []
            for b in range(bands):
                at_x = points_x[b][y : y + 1]
                found.append(
                    wave[b * points : (b + 1) * points]
                    + phase[0] * at_x
                    + phase[1] * swapped(at_x, -1.0)
                    + points_row[b][y : y + 1]
                )
            y_action(y, found)

    def spectrum(stage):
        def action(y, found):
            field = potential[y]
            product = jnp.concatenate([f * jnp.concatenate([field, field], 1) for f in found], 0)
            slotted = table_left(x_in_c, product) + table_left(x_in_s, swapped(product, 1.0))
            levels_r[pl.ds(y, rows + 8, stride=planes), :] = slotted[:, :points]
            levels_i[pl.ds(y, rows + 8, stride=planes), :] = slotted[:, points:]

        space(action)
        both = jnp.concatenate([levels_r[...], levels_i[...]], 1)
        found = table_right(both[0 : rows * planes], z_in).reshape(n, bands, slots, planes, points)
        sent[stage] = found
        for b in range(bands):
            start = (rows + b) * planes
            top = both[start : start + planes]
            zero = both[b * slots * planes : b * slots * planes + planes]
            last = table_right(zero, point_in[2])
            last = last * y_phase_c - turn(last) * y_phase_s
            sent[stage, home, b, 0] = (
                sent[stage, home, b, 0] * alone
                + table_right(top, point_in[0])
                + table_right(zero, point_in[1])
                + last
            )

    def pairs():
        return [(i, j) for i in range(bands) for j in range(bands)]

    def mixing(which, turn_at):
        total = jnp.sum(jnp.sum(grams_got[which], 0), 1, keepdims=True)
        square = bands * bands
        cc = {ij: total[k : k + 1] for k, ij in enumerate(pairs())}
        ca = {ij: total[square + k : square + k + 1] for k, ij in enumerate(pairs())}
        aa = {ij: total[2 * square + k : 2 * square + k + 1] for k, ij in enumerate(pairs())}
        factor = [1.0 + step_size * (ca[i, i] / (cc[i, i] + epsilon)) for i in range(bands)]
        moved = {
            (i, j): factor[i] * factor[j] * cc[i, j]
            - step_size * (factor[i] * ca[i, j] + factor[j] * ca[j, i])
            + step_size * step_size * aa[i, j]
            for i, j in pairs()
        }
        weights = []
        for b in range(bands):
            r = [rotations[turn_at, b, c] for c in range(bands)]
            length = sum(r[i] * r[j] * moved[i, j] for i, j in pairs())
            scale = lax.rsqrt(jnp.maximum(length, 0.0) + epsilon)
            weights.append([(scale * r[c] * factor[c], scale * r[c] * (-step_size)) for c in range(bands)])
        return weights

    y_outward(current, 0)
    exchange(0, None)
    mixed[...] = got[0]
    stage = 0
    for t in range(iters):
        spectrum(stage + 1)
        exchange(stage + 1, None)
        for b in range(bands):
            for x in range(slots):
                applied[b, x] = mask[x] * (
                    kinetic[x] * current[b, x] + y_inward(stage + 1, b, x) * (1.0 / points**3)
                )
        for k, (i, j) in enumerate(pairs()):
            for q, (u, v) in enumerate(((current, current), (current, applied), (applied, applied))):
                product = jnp.sum((u[i] * v[j]).reshape(slots * half, points), 0, keepdims=True)
                grams[t, q * bands * bands + k : q * bands * bands + k + 1, :] = product
        y_outward(applied, stage + 2)
        exchange(stage + 2, t)
        weights = mixing(t, t)
        old = [got[0, :, b] for b in range(bands)]
        new_mixed, new_current = [], []
        for b in range(bands):
            new_mixed.append(
                sum(weights[b][c][0] * old[c] + weights[b][c][1] * got[stage + 2, :, c] for c in range(bands))
            )
            new_current.append(
                sum(weights[b][c][0] * current[c] + weights[b][c][1] * applied[c] for c in range(bands))
            )
        for b in range(bands):
            current[b] = new_current[b]
            mixed[:, b] = new_mixed[b]
            got[0, :, b] = new_mixed[b]
        stage += 2

    def last_arrival(origin):
        place = new_out.at[:, pl.ds(lax.rem(plane_of(origin), planes), slots)]
        return pltpu.make_async_remote_copy(
            src_ref=current,
            dst_ref=place,
            send_sem=last_sem.at[0],
            recv_sem=last_sem.at[4 + lax.rem(plane_of(origin), planes) // slots],
            device_id=at(origin),
            device_id_type=MESH,
        )

    def last_sent():
        return pltpu.make_async_remote_copy(
            src_ref=current,
            dst_ref=new_out.at[:, pl.ds(lax.rem(plane_of(me), planes), slots)],
            send_sem=last_sem.at[0],
            recv_sem=last_sem.at[4 + lax.rem(plane_of(me), planes) // slots],
            device_id=at(source),
            device_id_type=MESH,
        )

    def last_own():
        return pltpu.make_async_copy(
            current, new_out.at[:, pl.ds(lax.rem(plane_of(me), planes), slots)], last_sem.at[0]
        )

    def point_back(target, sem):
        return pltpu.make_async_remote_copy(
            src_ref=current.at[:, 0, pl.ds(0, 8)],
            dst_ref=special_out,
            send_sem=last_sem.at[sem],
            recv_sem=last_sem.at[3],
            device_id=at(target),
            device_id_type=MESH,
        )

    @pl.when(source == me)
    def _():
        last_own().start()

    @pl.when(source != me)
    def _():
        last_sent().start()

    @pl.when(me == home)
    def _():
        point_back(0, 1).start()
        point_back(high_owner, 2).start()

    @pl.when(jnp.logical_and(me != 0, me != high_owner))
    def _():
        special_out[...] = jnp.zeros_like(special_out)

    @pl.when(jnp.logical_and(me * planes >= half // 2, me * planes < points - half // 2))
    def _():
        new_out[...] = jnp.zeros_like(new_out)

    def density(y, found):
        total = sum(f[:, :points] * f[:, :points] + f[:, points:] * f[:, points:] for f in found)
        part[y] = total * (2.0 / (bands * peers))

    space(density)

    def swap(i):
        return pltpu.make_async_remote_copy(
            src_ref=part,
            dst_ref=part_got.at[i - 1],
            send_sem=dens_sem.at[0, i - 1],
            recv_sem=dens_sem.at[1, i - 1],
            device_id={"band": lax.rem(band + i, peers), "grid": me},
            device_id_type=MESH,
        )

    for i in range(1, peers):
        swap(i).start()
    for i in range(1, peers):
        swap(i).wait()
    total = part[...] + core[...]
    for i in range(1, peers):
        total = total + part_got[i - 1]
    density_out[...] = total

    @pl.when(source == me)
    def _():
        last_own().wait()

    @pl.when(source != me)
    def _():
        last_sent().wait_send()

    @pl.when(me == home)
    def _():
        point_back(0, 1).wait_send()
        point_back(high_owner, 2).wait_send()

    @pl.when(jnp.logical_or(me == 0, me == high_owner))
    def _():
        point_back(home, 1).wait_recv()

    @pl.loop(0, n)
    def _(origin):
        @pl.when(jnp.logical_and(plane_of(origin) // planes == me, origin != me))
        def _():
            last_arrival(origin).wait_recv()


def update_bands(coefficients, potential, core, rotations):
    n, peers = lax.axis_size("grid"), lax.axis_size("band")
    bands, _, planes, points, _ = coefficients.shape
    iters = rotations.shape[0]
    half, quarter = points // 2, points // 4
    slots = half // n
    me = lax.axis_index("grid")

    def keep(value, axis):
        low = lax.slice_in_dim(value, 0, quarter, axis=axis)
        high = lax.slice_in_dim(value, points - quarter, points, axis=axis)
        return jnp.concatenate([low, high], axis)

    kept = keep(keep(coefficients, 3), 4)
    packed = jnp.concatenate([kept[:, 0], kept[:, 1]], -1)
    along_x = jnp.where(me == quarter // planes, coefficients[:, :, quarter % planes, 0, 0], 0.0)
    along_z = jnp.where(me == 0, coefficients[:, :, 0, 0, quarter], 0.0)
    along_y = jnp.where(me == 0, coefficients[:, :, 0, quarter, 0], 0.0)
    row = jnp.stack([jnp.zeros_like(along_x), along_x, along_z, along_y], -1)
    row = jnp.pad(row, ((0, 0), (0, 0), (0, half - 4))).reshape(bands, 1, points)
    lane = lax.iota(jnp.int32, points)
    zero_lane = (lane % half == 0).astype(F32)
    special = jnp.concatenate(
        [jnp.pad(row, ((0, 0), (0, 7), (0, 0))), jnp.broadcast_to(zero_lane, (bands, 8, points))], 1
    )

    def frequency(slot):
        return jnp.where(slot < quarter, slot, slot - half)

    gx = frequency(me * slots + lax.iota(jnp.int32, slots))[:, None, None]
    gy = frequency(lax.iota(jnp.int32, half))[None, :, None]
    gz = frequency(lane % half)[None, None, :]
    squared = gx * gx + gy * gy + gz * gz
    spot = (gx == -quarter) & (gy == 0) & (lane % half < 4)[None, None, :]
    squared = jnp.where(spot, quarter * quarter, squared)
    mask = (16 * squared <= points * points).astype(F32)
    kinetic = kinetic_scale * squared.astype(F32) / (points * points)

    rows = bands * half
    vmem = pl.BlockSpec(memory_space=pltpu.VMEM)
    smem = pl.BlockSpec(memory_space=pltpu.SMEM)
    stages = 2 * iters + 1
    chunk = (bands, slots, planes, points)
    gram_rows = -(-3 * bands * bands // 8) * 8
    dma = pltpu.SemaphoreType.DMA
    tables = band_tables(n, bands, points)
    y_phase = lax.dynamic_slice_in_dim(jnp.asarray(tables[-1]), me * planes, planes, 1)
    new, back, density = pl.pallas_call(
        functools.partial(band_kernel, n, peers, bands, points, iters),
        out_shape=(
            jax.ShapeDtypeStruct((bands, planes, half, points), F32),
            jax.ShapeDtypeStruct((bands, 8, points), F32),
            jax.ShapeDtypeStruct((planes, points, points), F32),
        ),
        in_specs=[vmem] * 6 + [smem] + [vmem] * (len(tables) + 1),
        out_specs=(vmem, vmem, vmem),
        scratch_shapes=[
            pltpu.VMEM((bands, slots, half, points), F32),
            pltpu.VMEM((bands, slots, half, points), F32),
            pltpu.VMEM((stages, n) + chunk, F32),
            pltpu.VMEM((stages, n) + chunk, F32),
            pltpu.VMEM((iters, gram_rows, points), F32),
            pltpu.VMEM((iters, n, gram_rows, points), F32),
            pltpu.VMEM(((rows + 8) * planes, points), F32),
            pltpu.VMEM(((rows + 8) * planes, points), F32),
            pltpu.VMEM((n,) + chunk, F32),
            pltpu.VMEM((2, bands, 16, points), F32),
            pltpu.VMEM((planes, points, points), F32),
            pltpu.VMEM((max(peers - 1, 1), planes, points, points), F32),
            dma((stages, n)),
            dma((stages, n)),
            dma((iters, n)),
            dma((iters, n)),
            dma((5 + planes // slots,)),
            dma((4 + planes // slots,)),
            dma((2, max(peers - 1, 1))),
        ],
        compiler_params=pltpu.CompilerParams(
            collective_id=0, has_side_effects=True, vmem_limit_bytes=60 * 2**20
        ),
    )(packed, special, mask, kinetic, potential, core, rotations, *tables, y_phase)

    parts = jnp.stack([new[..., :half], new[..., half:]], 1)

    def widen(value, axis):
        low = lax.slice_in_dim(value, 0, quarter, axis=axis)
        high = lax.slice_in_dim(value, quarter, half, axis=axis)
        shape = list(value.shape)
        shape[axis] = points - half
        return jnp.concatenate([low, jnp.zeros(shape, F32), high], axis)

    gx_own = me * planes + lax.iota(jnp.int32, planes)
    live = (gx_own != points - quarter)[:, None, None] | (
        (lax.iota(jnp.int32, half) == 0)[None, :, None] & (lax.iota(jnp.int32, half) == 0)[None, None, :]
    )
    kept_plane = ((gx_own < quarter) | (gx_own >= points - quarter))[:, None, None]
    wide = widen(widen(jnp.where(live & kept_plane, parts, 0.0), 3), 4)
    found = back[:, 0].reshape(bands, 2, half)
    i_x = lax.broadcasted_iota(jnp.int32, (1, 1, planes, points, points), 2) + me * planes
    i_y = lax.broadcasted_iota(jnp.int32, (1, 1, planes, points, points), 3)
    i_z = lax.broadcasted_iota(jnp.int32, (1, 1, planes, points, points), 4)

    def spread(k):
        return found[:, :, k][:, :, None, None, None]

    wide = jnp.where((i_x == quarter) & (i_y == 0) & (i_z == 0), spread(1), wide)
    wide = jnp.where((i_x == 0) & (i_y == 0) & (i_z == quarter), spread(2), wide)
    wide = jnp.where((i_x == 0) & (i_y == quarter) & (i_z == 0), spread(3), wide)
    return wide, density


def frequencies(points, offset, length):
    places = offset + lax.iota(jnp.int32, length)
    return jnp.where(2 * places < points, places, places - points)


def reciprocal_tables(points, offset, length):
    along_x = frequencies(points, offset, length)
    along = frequencies(points, 0, points)
    squared = (
        along_x[:, None, None] * along_x[:, None, None]
        + along[None, :, None] * along[None, :, None]
        + along[None, None, :] * along[None, None, :]
    )
    return jnp.where(
        squared > 0, coulomb_scale * (points * points) / jnp.maximum(squared, 1).astype(F32), 0.0
    )


def full_dot(a, b):
    return jnp.dot(a, b, preferred_element_type=F32, precision=lax.Precision.HIGHEST)


def field_kernel(
    n, points, hidden,
    density, cube, external, coulomb, basis, slope, slope_t, mlp_in, mlp_out, out,
    sent, got, back_h, back_y, got_h, got_y, send_sem, recv_sem,
):
    me = lax.axis_index("grid")
    band = lax.axis_index("band")
    planes = points // n
    block = planes * planes

    barrier = pltpu.get_barrier_semaphore()

    @pl.loop(1, n)
    def _(i):
        pl.semaphore_signal(
            barrier, inc=1, device_id={"band": band, "grid": lax.rem(me + i, n)}, device_id_type=MESH
        )

    def exchange(pairs):
        def copy(k, target, origin):
            source, place = pairs[k][1:]
            return pltpu.make_async_remote_copy(
                src_ref=source.at[target],
                dst_ref=place.at[pl.ds(origin * block, block)],
                send_sem=send_sem.at[pairs[k][0], target],
                recv_sem=recv_sem.at[pairs[k][0], origin],
                device_id={"band": band, "grid": target},
                device_id_type=MESH,
            )

        @pl.loop(1, n)
        def _(i):
            for k in range(len(pairs)):
                copy(k, lax.rem(me + i, n), me).start()

        for stage, source, place in pairs:
            own = pltpu.make_async_copy(
                source.at[me], place.at[pl.ds(me * block, block)], recv_sem.at[stage, me]
            )
            own.start()
            own.wait()

        @pl.loop(1, n)
        def _(i):
            origin = lax.rem(me + n - i, n)
            for k in range(len(pairs)):
                copy(k, lax.rem(me + i, n), me).wait_send()
                copy(k, origin, origin).wait_recv()

    for y in range(planes):
        level = full_dot(full_dot(basis[...], density[y] - 2.275), basis[...])
        out[pl.ds(y, points, stride=planes), :] = level
    sent[...] = out[...].reshape(n, block, points)
    pl.semaphore_wait(barrier, n - 1)
    exchange([(0, sent, got)])
    arrived = got[...].reshape(n, planes, planes, points)
    for x in range(planes):
        column = arrived[:, x].reshape(points, points)
        weighted = coulomb[x] * full_dot(basis[...], column)
        back_h[:, x * planes : (x + 1) * planes] = full_dot(basis[...], weighted).reshape(n, planes, points)
        back_y[:, x * planes : (x + 1) * planes] = full_dot(slope[...], column).reshape(n, planes, points)
    exchange([(1, back_h, got_h), (2, back_y, got_y)])

    for y in range(planes):
        hartree = full_dot(full_dot(basis[...], got_h[pl.ds(y, points, stride=planes), :]), basis[...])
        change_y = full_dot(full_dot(basis[...], got_y[pl.ds(y, points, stride=planes), :]), basis[...])
        change_y = change_y * (1.0 / (points * points))
        varying = density[y] - 2.275
        change_x = full_dot(slope[...], varying)
        change_z = full_dot(varying, slope_t[...])
        gradient = jnp.sqrt(change_x * change_x + change_y * change_y + change_z * change_z)
        root = cube[y]
        reduced = gradient / (reduced_scale * density[y] * root)
        bounded = reduced / (1.0 + reduced)

        def unit(k, total):
            return total + mlp_out[k] * jnp.tanh(mlp_in[0, k] * root + mlp_in[1, k] * bounded + mlp_in[2, k])

        enhance = lax.fori_loop(0, hidden, unit, jnp.ones_like(root))
        out[y * points : (y + 1) * points, :] = (
            external[y] + hartree - exchange_scale * root * enhance
        )


def body(coefficients, potential, external, core_density, rotations, mlp_in, mlp_out):
    points = potential.shape[1]
    planes = coefficients.shape[2]
    n = lax.axis_size("grid")
    offset = lax.axis_index("grid") * planes
    coulomb = reciprocal_tables(points, offset, planes) * (1.0 / points**3)
    current, density = update_bands(coefficients, potential, core_density, rotations)

    cell = np.arange(points)
    angle = 2.0 * np.pi * ((cell[:, None] * cell[None, :]) % points) / points
    freq = np.where(2 * cell < points, cell, cell - points)
    slope = gradient_scale * np.where(2 * freq == -points, 0, freq) / points
    back = (np.exp(1j * angle) * slope[None, :] * 1j) @ np.exp(-1j * angle) / points
    slope_table = np.ascontiguousarray(back.real).astype(np.float32)
    basis = (np.cos(angle) + np.sin(angle)).astype(np.float32)
    vmem = pl.BlockSpec(memory_space=pltpu.VMEM)
    smem = pl.BlockSpec(memory_space=pltpu.SMEM)
    block = planes * planes
    new_potential = pl.pallas_call(
        functools.partial(field_kernel, n, points, mlp_out.shape[0]),
        out_shape=jax.ShapeDtypeStruct((planes * points, points), F32),
        in_specs=[vmem] * 7 + [smem, smem],
        out_specs=vmem,
        scratch_shapes=[
            pltpu.VMEM((n, block, points), F32),
            pltpu.VMEM((n * block, points), F32),
            pltpu.VMEM((n, block, points), F32),
            pltpu.VMEM((n, block, points), F32),
            pltpu.VMEM((n * block, points), F32),
            pltpu.VMEM((n * block, points), F32),
            pltpu.SemaphoreType.DMA((3, n)),
            pltpu.SemaphoreType.DMA((3, n)),
        ],
        compiler_params=pltpu.CompilerParams(
            collective_id=1, has_side_effects=True, vmem_limit_bytes=40 * 2**20
        ),
    )(density, jnp.cbrt(density), external, coulomb, basis, slope_table, slope_table.T.copy(), mlp_in, mlp_out)
    return (current, new_potential.reshape(planes, points, points))


def solution(mesh):
    in_specs = (
        P("band", None, "grid", None, None),
        P("grid", None, None),
        P("grid", None, None),
        P("grid", None, None),
        P(None, "band", None),
        P(),
        P(),
    )
    out_specs = (P("band", None, "grid", None, None), P("grid", None, None))
    return jax.shard_map(body, mesh=mesh, in_specs=in_specs, out_specs=out_specs, check_vma=False)
```

```python
import functools
import math

import jax
import jax.numpy as jnp
import numpy as np
from jax import lax
from jax.experimental import pallas as pl
from jax.experimental.pallas import tpu as pltpu
from jax.sharding import PartitionSpec as P

MESH = pl.DeviceIdType.MESH
F32 = jnp.float32
BF16 = jnp.bfloat16

step_size = 0.2
epsilon = 1e-06
spacing = 0.58
kinetic_scale = 0.5 * (2.0 * math.pi / spacing) ** 2
coulomb_scale = spacing * spacing / math.pi
gradient_scale = 2.0 * math.pi / spacing
reduced_scale = 2.0 * (3.0 * math.pi * math.pi) ** (1.0 / 3.0)
exchange_scale = (3.0 / math.pi) ** (1.0 / 3.0)


def halves(table):
    table = np.asarray(table, np.float32)
    high = table.astype(BF16)
    low = (table - high.astype(np.float32)).astype(BF16)
    return np.stack([high, low])


def split(value):
    high = value.astype(BF16)
    return high, (value - high.astype(F32)).astype(BF16)


def dot(a, b):
    return jnp.dot(a, b, preferred_element_type=F32)


def table_left(table, value):
    high, low = split(value)
    return dot(table[0], high) + (dot(table[0], low) + dot(table[1], high))


def table_right(value, table):
    high, low = split(value)
    return dot(high, table[0]) + (dot(low, table[0]) + dot(high, table[1]))


def band_tables(n, bands, points):
    half = points // 2
    slots = half // n
    keep = np.arange(half)
    keep = np.where(keep < half // 2, keep, keep - half)
    cell = np.arange(points)
    angle = 2.0 * np.pi * ((keep[:, None] * cell[None, :]) % points) / points
    cos, sin = np.cos(angle), np.sin(angle)
    top = 2.0 * np.pi * ((half // 2 * cell) % points) / points
    ctop, stop = np.cos(top), np.sin(top)
    y_out = np.concatenate([cos.T, sin.T], 1)
    y_in = np.concatenate([cos, sin], 1)
    z_out = np.block([[cos, sin], [-sin, cos]])
    z_in = np.block([[cos.T, -sin.T], [sin.T, cos.T]])
    rows = bands * half
    x_cos = np.zeros((bands, points, n, bands, slots))
    x_sin = np.zeros_like(x_cos)
    for b in range(bands):
        x_cos[b, :, :, b] = cos.T.reshape(points, n, slots)
        x_sin[b, :, :, b] = sin.T.reshape(points, n, slots)
    x_cos = x_cos.reshape(bands * points, rows)
    x_sin = x_sin.reshape(bands * points, rows)
    x_out = np.concatenate([x_cos, x_sin], 1)
    extra = np.zeros((2, 8, bands * points))
    for b in range(bands):
        extra[0, b, b * points : (b + 1) * points] = ctop
        extra[1, b, b * points : (b + 1) * points] = stop
    x_in = np.stack([np.concatenate([x_cos.T, extra[0]]), np.concatenate([x_sin.T, extra[1]])])
    ones, zeros = np.ones(points), np.zeros(points)
    point_out = np.zeros((3, points, 2 * points))
    point_in = np.zeros((3, 2 * points, points))
    for i, (c, s) in enumerate(((ones, zeros), (ctop, stop), (ones, zeros))):
        point_out[i, i + 1] = np.concatenate([c, s])
        point_out[i, half + i + 1] = np.concatenate([-s, c])
        point_in[i, :, i + 1] = np.concatenate([c, s])
        point_in[i, :, half + i + 1] = np.concatenate([-s, c])
    return [halves(t) for t in (y_out, y_in, z_out, z_in, x_out, x_in[0], x_in[1])] + [
        np.moveaxis(halves(point_out), 1, 0),
        np.moveaxis(halves(point_in), 1, 0),
        np.stack([ctop, stop]).astype(np.float32)[:, :, None],
    ]


def band_kernel(
    n, peers, bands, points, iters,
    packed, special, mask, kinetic, potential, core, rotations,
    y_out, y_in, z_out, z_in, x_out, x_in_c, x_in_s, point_out, point_in, phase, y_phase,
    new_out, special_out, density_out,
    current, applied, sent, got, grams, grams_got, levels_r, levels_i, mixed,
    special_got, part, part_got, send_sem, recv_sem, gram_send, gram_recv, first_sem, last_sem, dens_sem,
):
    me = lax.axis_index("grid")
    band = lax.axis_index("band")
    half = points // 2
    slots = half // n
    planes = points // n
    rows = bands * half
    home = n // 2
    high_owner = (half // 2) // planes

    def at(grid):
        return {"band": band, "grid": grid}

    barrier = pltpu.get_barrier_semaphore()

    @pl.loop(1, n)
    def _(i):
        pl.semaphore_signal(barrier, inc=1, device_id=at(lax.rem(me + i, n)), device_id_type=MESH)

    for i in range(1, peers):
        pl.semaphore_signal(
            barrier, inc=1, device_id={"band": lax.rem(band + i, peers), "grid": me}, device_id_type=MESH
        )
    pl.semaphore_wait(barrier, n - 1 + peers - 1)

    def plane_of(device):
        slot = device * slots
        return jnp.where(slot < half // 2, slot, slot + half)

    def first_copy(target):
        start = plane_of(target)
        return pltpu.make_async_remote_copy(
            src_ref=packed.at[:, pl.ds(lax.rem(start, planes), slots)],
            dst_ref=current,
            send_sem=first_sem.at[5 + lax.rem(start, planes) // slots],
            recv_sem=first_sem.at[1],
            device_id=at(target),
            device_id_type=MESH,
        )

    def first_own():
        return pltpu.make_async_copy(
            packed.at[:, pl.ds(lax.rem(plane_of(me), planes), slots)], current, first_sem.at[1]
        )

    def point_copy(place):
        return pltpu.make_async_remote_copy(
            src_ref=special,
            dst_ref=special_got.at[place],
            send_sem=first_sem.at[place * 2],
            recv_sem=first_sem.at[3 + place],
            device_id=at(home),
            device_id_type=MESH,
        )

    source = plane_of(me) // planes

    @pl.when(source == me)
    def _():
        first_own().start()

    @pl.loop(0, n)
    def _(target):
        @pl.when(jnp.logical_and(plane_of(target) // planes == me, target != me))
        def _():
            first_copy(target).start()

    @pl.when(me == 0)
    def _():
        point_copy(0).start()

    @pl.when(me == high_owner)
    def _():
        point_copy(1).start()

    @pl.loop(0, n)
    def _(target):
        @pl.when(jnp.logical_and(plane_of(target) // planes == me, target != me))
        def _():
            first_copy(target).wait_send()

    @pl.when(me == 0)
    def _():
        point_copy(0).wait_send()

    @pl.when(me == high_owner)
    def _():
        point_copy(1).wait_send()

    @pl.when(source == me)
    def _():
        first_own().wait()

    @pl.when(source != me)
    def _():
        first_copy(me).wait_recv()

    @pl.when(me == home)
    def _():
        point_copy(0).wait_recv()
        point_copy(1).wait_recv()
        for b in range(bands):
            current[b, 0, 0:8, :] = current[b, 0, 0:8, :] * mask[0, 0:8, :] * special[0, 8:16, :] + (
                special_got[0, b, 0:8, :] + special_got[1, b, 0:8, :]
            )

    for b in range(bands):
        current[b] = current[b] * mask[...]

    lanes = lax.broadcasted_iota(jnp.int32, (1, points), 1)
    sign = jnp.where(lanes < half, -1.0, 1.0).astype(F32)
    alone = jnp.where(lax.rem(lanes, half) == 0, 1.0, 0.0).astype(F32)

    def turn(value):
        return pltpu.roll(value, half, 1) * sign

    def exchange(stage, with_gram):
        def copies(target, origin):
            found = [
                pltpu.make_async_remote_copy(
                    src_ref=sent.at[stage, target],
                    dst_ref=got.at[stage, origin],
                    send_sem=send_sem.at[stage, target],
                    recv_sem=recv_sem.at[stage, origin],
                    device_id=at(target),
                    device_id_type=MESH,
                )
            ]
            if with_gram is not None:
                found.append(
                    pltpu.make_async_remote_copy(
                        src_ref=grams.at[with_gram],
                        dst_ref=grams_got.at[with_gram, origin],
                        send_sem=gram_send.at[with_gram, target],
                        recv_sem=gram_recv.at[with_gram, origin],
                        device_id=at(target),
                        device_id_type=MESH,
                    )
                )
            return found

        @pl.loop(1, n)
        def _(i):
            for copy in copies(lax.rem(me + i, n), me):
                copy.start()

        own = pltpu.make_async_copy(sent.at[stage, me], got.at[stage, me], recv_sem.at[stage, me])
        own.start()
        if with_gram is not None:
            mine = pltpu.make_async_copy(
                grams.at[with_gram], grams_got.at[with_gram, me], gram_recv.at[with_gram, me]
            )
            mine.start()
            mine.wait()
        own.wait()

        @pl.loop(1, n)
        def _(i):
            for copy in copies(lax.rem(me + i, n), me):
                copy.wait_send()
            origin = lax.rem(me + n - i, n)
            for copy in copies(origin, origin):
                copy.wait_recv()

    def y_outward(source_ref, stage):
        for b in range(bands):
            for x in range(slots):
                value = source_ref[b, x]
                full = table_left(y_out, jnp.concatenate([value, turn(value)], 0))
                sent[stage, :, b, x] = full.reshape(n, planes, points)

    def y_inward(stage, b, x):
        value = got[stage, :, b, x].reshape(points, points)
        return table_left(y_in, jnp.concatenate([value, -turn(value)], 0))

    def swapped(value, s):
        return jnp.concatenate([s * value[:, points:], -s * value[:, :points]], 1)

    y_phase_c = y_phase[0]
    y_phase_s = y_phase[1]

    def space(y_action):
        points_x, points_row = [], []
        for b in range(bands):
            row = mixed[home, b, 0]
            points_x.append(table_right(row, point_out[0]))
            along_z = table_right(row, point_out[1])
            along_y = table_right(row, point_out[2])
            points_row.append(along_z + along_y * y_phase_c + swapped(along_y, -1.0) * y_phase_s)
            mixed[home, b, 0] = row * alone
        levels = table_right(mixed[...].reshape(rows * planes, points), z_out)
        levels_r[0 : rows * planes, :] = levels[:, :points]
        levels_i[0 : rows * planes, :] = levels[:, points:]
        for y in range(planes):
            real = levels_r[pl.ds(y, rows, stride=planes), :]
            imag = levels_i[pl.ds(y, rows, stride=planes), :]
            stacked = jnp.concatenate(
                [jnp.concatenate([real, imag], 1), jnp.concatenate([-imag, real], 1)], 0
            )
            wave = table_left(x_out, stacked)
            found = []
            for b in range(bands):
                at_x = points_x[b][y : y + 1]
                found.append(
                    wave[b * points : (b + 1) * points]
                    + phase[0] * at_x
                    + phase[1] * swapped(at_x, -1.0)
                    + points_row[b][y : y + 1]
                )
            y_action(y, found)

    def spectrum(stage):
        def action(y, found):
            field = potential[y]
            product = jnp.concatenate([f * jnp.concatenate([field, field], 1) for f in found], 0)
            slotted = table_left(x_in_c, product) + table_left(x_in_s, swapped(product, 1.0))
            levels_r[pl.ds(y, rows + 8, stride=planes), :] = slotted[:, :points]
            levels_i[pl.ds(y, rows + 8, stride=planes), :] = slotted[:, points:]

        space(action)
        both = jnp.concatenate([levels_r[...], levels_i[...]], 1)
        found = table_right(both[0 : rows * planes], z_in).reshape(n, bands, slots, planes, points)
        sent[stage] = found
        for b in range(bands):
            start = (rows + b) * planes
            top = both[start : start + planes]
            zero = both[b * slots * planes : b * slots * planes + planes]
            last = table_right(zero, point_in[2])
            last = last * y_phase_c - turn(last) * y_phase_s
            sent[stage, home, b, 0] = (
                sent[stage, home, b, 0] * alone
                + table_right(top, point_in[0])
                + table_right(zero, point_in[1])
                + last
            )

    def pairs():
        return [(i, j) for i in range(bands) for j in range(bands)]

    def mixing(which, turn_at):
        total = jnp.sum(jnp.sum(grams_got[which], 0), 1, keepdims=True)
        square = bands * bands
        cc = {ij: total[k : k + 1] for k, ij in enumerate(pairs())}
        ca = {ij: total[square + k : square + k + 1] for k, ij in enumerate(pairs())}
        aa = {ij: total[2 * square + k : 2 * square + k + 1] for k, ij in enumerate(pairs())}
        factor = [1.0 + step_size * (ca[i, i] / (cc[i, i] + epsilon)) for i in range(bands)]
        moved = {
            (i, j): factor[i] * factor[j] * cc[i, j]
            - step_size * (factor[i] * ca[i, j] + factor[j] * ca[j, i])
            + step_size * step_size * aa[i, j]
            for i, j in pairs()
        }
        weights = []
        for b in range(bands):
            r = [rotations[turn_at, b, c] for c in range(bands)]
            length = sum(r[i] * r[j] * moved[i, j] for i, j in pairs())
            scale = lax.rsqrt(jnp.maximum(length, 0.0) + epsilon)
            weights.append([(scale * r[c] * factor[c], scale * r[c] * (-step_size)) for c in range(bands)])
        return weights

    y_outward(current, 0)
    exchange(0, None)
    mixed[...] = got[0]
    stage = 0
    for t in range(iters):
        spectrum(stage + 1)
        exchange(stage + 1, None)
        for b in range(bands):
            for x in range(slots):
                applied[b, x] = mask[x] * (
                    kinetic[x] * current[b, x] + y_inward(stage + 1, b, x) * (1.0 / points**3)
                )
        for k, (i, j) in enumerate(pairs()):
            for q, (u, v) in enumerate(((current, current), (current, applied), (applied, applied))):
                product = jnp.sum((u[i] * v[j]).reshape(slots * half, points), 0, keepdims=True)
                grams[t, q * bands * bands + k : q * bands * bands + k + 1, :] = product
        y_outward(applied, stage + 2)
        exchange(stage + 2, t)
        weights = mixing(t, t)
        old = [got[0, :, b] for b in range(bands)]
        new_mixed, new_current = [], []
        for b in range(bands):
            new_mixed.append(
                sum(weights[b][c][0] * old[c] + weights[b][c][1] * got[stage + 2, :, c] for c in range(bands))
            )
            new_current.append(
                sum(weights[b][c][0] * current[c] + weights[b][c][1] * applied[c] for c in range(bands))
            )
        for b in range(bands):
            current[b] = new_current[b]
            mixed[:, b] = new_mixed[b]
            got[0, :, b] = new_mixed[b]
        stage += 2

    def last_arrival(origin):
        place = new_out.at[:, pl.ds(lax.rem(plane_of(origin), planes), slots)]
        return pltpu.make_async_remote_copy(
            src_ref=current,
            dst_ref=place,
            send_sem=last_sem.at[0],
            recv_sem=last_sem.at[4 + lax.rem(plane_of(origin), planes) // slots],
            device_id=at(origin),
            device_id_type=MESH,
        )

    def last_sent():
        return pltpu.make_async_remote_copy(
            src_ref=current,
            dst_ref=new_out.at[:, pl.ds(lax.rem(plane_of(me), planes), slots)],
            send_sem=last_sem.at[0],
            recv_sem=last_sem.at[4 + lax.rem(plane_of(me), planes) // slots],
            device_id=at(source),
            device_id_type=MESH,
        )

    def last_own():
        return pltpu.make_async_copy(
            current, new_out.at[:, pl.ds(lax.rem(plane_of(me), planes), slots)], last_sem.at[0]
        )

    def point_back(target, sem):
        return pltpu.make_async_remote_copy(
            src_ref=current.at[:, 0, pl.ds(0, 8)],
            dst_ref=special_out,
            send_sem=last_sem.at[sem],
            recv_sem=last_sem.at[3],
            device_id=at(target),
            device_id_type=MESH,
        )

    @pl.when(source == me)
    def _():
        last_own().start()

    @pl.when(source != me)
    def _():
        last_sent().start()

    @pl.when(me == home)
    def _():
        point_back(0, 1).start()
        point_back(high_owner, 2).start()

    @pl.when(jnp.logical_and(me != 0, me != high_owner))
    def _():
        special_out[...] = jnp.zeros_like(special_out)

    @pl.when(jnp.logical_and(me * planes >= half // 2, me * planes < points - half // 2))
    def _():
        new_out[...] = jnp.zeros_like(new_out)

    def density(y, found):
        total = sum(f[:, :points] * f[:, :points] + f[:, points:] * f[:, points:] for f in found)
        part[y] = total * (2.0 / (bands * peers))

    space(density)

    def swap(i):
        return pltpu.make_async_remote_copy(
            src_ref=part,
            dst_ref=part_got.at[i - 1],
            send_sem=dens_sem.at[0, i - 1],
            recv_sem=dens_sem.at[1, i - 1],
            device_id={"band": lax.rem(band + i, peers), "grid": me},
            device_id_type=MESH,
        )

    for i in range(1, peers):
        swap(i).start()
    for i in range(1, peers):
        swap(i).wait()
    total = part[...] + core[...]
    for i in range(1, peers):
        total = total + part_got[i - 1]
    density_out[...] = total

    @pl.when(source == me)
    def _():
        last_own().wait()

    @pl.when(source != me)
    def _():
        last_sent().wait_send()

    @pl.when(me == home)
    def _():
        point_back(0, 1).wait_send()
        point_back(high_owner, 2).wait_send()

    @pl.when(jnp.logical_or(me == 0, me == high_owner))
    def _():
        point_back(home, 1).wait_recv()

    @pl.loop(0, n)
    def _(origin):
        @pl.when(jnp.logical_and(plane_of(origin) // planes == me, origin != me))
        def _():
            last_arrival(origin).wait_recv()


def update_bands(coefficients, potential, core, rotations):
    n, peers = lax.axis_size("grid"), lax.axis_size("band")
    bands, _, planes, points, _ = coefficients.shape
    iters = rotations.shape[0]
    half, quarter = points // 2, points // 4
    slots = half // n
    me = lax.axis_index("grid")

    def keep(value, axis):
        low = lax.slice_in_dim(value, 0, quarter, axis=axis)
        high = lax.slice_in_dim(value, points - quarter, points, axis=axis)
        return jnp.concatenate([low, high], axis)

    kept = keep(keep(coefficients, 3), 4)
    packed = jnp.concatenate([kept[:, 0], kept[:, 1]], -1)
    along_x = jnp.where(me == quarter // planes, coefficients[:, :, quarter % planes, 0, 0], 0.0)
    along_z = jnp.where(me == 0, coefficients[:, :, 0, 0, quarter], 0.0)
    along_y = jnp.where(me == 0, coefficients[:, :, 0, quarter, 0], 0.0)
    row = jnp.stack([jnp.zeros_like(along_x), along_x, along_z, along_y], -1)
    row = jnp.pad(row, ((0, 0), (0, 0), (0, half - 4))).reshape(bands, 1, points)
    lane = lax.iota(jnp.int32, points)
    zero_lane = (lane % half == 0).astype(F32)
    special = jnp.concatenate(
        [jnp.pad(row, ((0, 0), (0, 7), (0, 0))), jnp.broadcast_to(zero_lane, (bands, 8, points))], 1
    )

    def frequency(slot):
        return jnp.where(slot < quarter, slot, slot - half)

    gx = frequency(me * slots + lax.iota(jnp.int32, slots))[:, None, None]
    gy = frequency(lax.iota(jnp.int32, half))[None, :, None]
    gz = frequency(lane % half)[None, None, :]
    squared = gx * gx + gy * gy + gz * gz
    spot = (gx == -quarter) & (gy == 0) & (lane % half < 4)[None, None, :]
    squared = jnp.where(spot, quarter * quarter, squared)
    mask = (16 * squared <= points * points).astype(F32)
    kinetic = kinetic_scale * squared.astype(F32) / (points * points)

    rows = bands * half
    vmem = pl.BlockSpec(memory_space=pltpu.VMEM)
    smem = pl.BlockSpec(memory_space=pltpu.SMEM)
    stages = 2 * iters + 1
    chunk = (bands, slots, planes, points)
    gram_rows = -(-3 * bands * bands // 8) * 8
    dma = pltpu.SemaphoreType.DMA
    tables = band_tables(n, bands, points)
    y_phase = lax.dynamic_slice_in_dim(jnp.asarray(tables[-1]), me * planes, planes, 1)
    new, back, density = pl.pallas_call(
        functools.partial(band_kernel, n, peers, bands, points, iters),
        out_shape=(
            jax.ShapeDtypeStruct((bands, planes, half, points), F32),
            jax.ShapeDtypeStruct((bands, 8, points), F32),
            jax.ShapeDtypeStruct((planes, points, points), F32),
        ),
        in_specs=[vmem] * 6 + [smem] + [vmem] * (len(tables) + 1),
        out_specs=(vmem, vmem, vmem),
        scratch_shapes=[
            pltpu.VMEM((bands, slots, half, points), F32),
            pltpu.VMEM((bands, slots, half, points), F32),
            pltpu.VMEM((stages, n) + chunk, F32),
            pltpu.VMEM((stages, n) + chunk, F32),
            pltpu.VMEM((iters, gram_rows, points), F32),
            pltpu.VMEM((iters, n, gram_rows, points), F32),
            pltpu.VMEM(((rows + 8) * planes, points), F32),
            pltpu.VMEM(((rows + 8) * planes, points), F32),
            pltpu.VMEM((n,) + chunk, F32),
            pltpu.VMEM((2, bands, 16, points), F32),
            pltpu.VMEM((planes, points, points), F32),
            pltpu.VMEM((max(peers - 1, 1), planes, points, points), F32),
            dma((stages, n)),
            dma((stages, n)),
            dma((iters, n)),
            dma((iters, n)),
            dma((5 + planes // slots,)),
            dma((4 + planes // slots,)),
            dma((2, max(peers - 1, 1))),
        ],
        compiler_params=pltpu.CompilerParams(
            collective_id=0, has_side_effects=True, vmem_limit_bytes=60 * 2**20
        ),
    )(packed, special, mask, kinetic, potential, core, rotations, *tables, y_phase)

    parts = jnp.stack([new[..., :half], new[..., half:]], 1)

    def widen(value, axis):
        low = lax.slice_in_dim(value, 0, quarter, axis=axis)
        high = lax.slice_in_dim(value, quarter, half, axis=axis)
        shape = list(value.shape)
        shape[axis] = points - half
        return jnp.concatenate([low, jnp.zeros(shape, F32), high], axis)

    gx_own = me * planes + lax.iota(jnp.int32, planes)
    live = (gx_own != points - quarter)[:, None, None] | (
        (lax.iota(jnp.int32, half) == 0)[None, :, None] & (lax.iota(jnp.int32, half) == 0)[None, None, :]
    )
    kept_plane = ((gx_own < quarter) | (gx_own >= points - quarter))[:, None, None]
    wide = widen(widen(jnp.where(live & kept_plane, parts, 0.0), 3), 4)
    found = back[:, 0].reshape(bands, 2, half)
    i_x = lax.broadcasted_iota(jnp.int32, (1, 1, planes, points, points), 2) + me * planes
    i_y = lax.broadcasted_iota(jnp.int32, (1, 1, planes, points, points), 3)
    i_z = lax.broadcasted_iota(jnp.int32, (1, 1, planes, points, points), 4)

    def spread(k):
        return found[:, :, k][:, :, None, None, None]

    wide = jnp.where((i_x == quarter) & (i_y == 0) & (i_z == 0), spread(1), wide)
    wide = jnp.where((i_x == 0) & (i_y == 0) & (i_z == quarter), spread(2), wide)
    wide = jnp.where((i_x == 0) & (i_y == quarter) & (i_z == 0), spread(3), wide)
    return wide, density


def frequencies(points, offset, length):
    places = offset + lax.iota(jnp.int32, length)
    return jnp.where(2 * places < points, places, places - points)


def reciprocal_tables(points, offset, length):
    along_x = frequencies(points, offset, length)
    along = frequencies(points, 0, points)
    squared = (
        along_x[:, None, None] * along_x[:, None, None]
        + along[None, :, None] * along[None, :, None]
        + along[None, None, :] * along[None, None, :]
    )
    return jnp.where(
        squared > 0, coulomb_scale * (points * points) / jnp.maximum(squared, 1).astype(F32), 0.0
    )


def full_dot(a, b):
    return jnp.dot(a, b, preferred_element_type=F32, precision=lax.Precision.HIGHEST)


def field_kernel(
    n, peers, points, hidden,
    density, cube, external, coulomb, basis, basis_2, slope_2, slope_t2, mlp_in, mlp_out, out,
    staged, sent, got, back_h, back_y, got_h, got_y, send_sem, recv_sem, share_sem,
):
    me = lax.axis_index("grid")
    band = lax.axis_index("band")
    planes = points // n
    block = planes * planes

    barrier = pltpu.get_barrier_semaphore()

    @pl.loop(1, n)
    def _(i):
        pl.semaphore_signal(
            barrier, inc=1, device_id={"band": band, "grid": lax.rem(me + i, n)}, device_id_type=MESH
        )

    share = planes // peers if planes % peers == 0 else planes
    others = range(1, peers) if share < planes else range(0)
    for i in others:
        pl.semaphore_signal(
            barrier, inc=1, device_id={"band": lax.rem(band + i, peers), "grid": me}, device_id_type=MESH
        )

    def exchange(pairs):
        def copy(k, target, origin):
            source, place = pairs[k][1:]
            return pltpu.make_async_remote_copy(
                src_ref=source.at[target],
                dst_ref=place.at[pl.ds(origin * block, block)],
                send_sem=send_sem.at[pairs[k][0], target],
                recv_sem=recv_sem.at[pairs[k][0], origin],
                device_id={"band": band, "grid": target},
                device_id_type=MESH,
            )

        @pl.loop(1, n)
        def _(i):
            for k in range(len(pairs)):
                copy(k, lax.rem(me + i, n), me).start()

        for stage, source, place in pairs:
            own = pltpu.make_async_copy(
                source.at[me], place.at[pl.ds(me * block, block)], recv_sem.at[stage, me]
            )
            own.start()
            own.wait()

        @pl.loop(1, n)
        def _(i):
            origin = lax.rem(me + n - i, n)
            for k in range(len(pairs)):
                copy(k, lax.rem(me + i, n), me).wait_send()
                copy(k, origin, origin).wait_recv()

    for y in range(planes):
        level = full_dot(full_dot(basis[...], density[y] - 2.275), basis[...])
        staged[pl.ds(y, points, stride=planes), :] = level
    sent[...] = staged[...].reshape(n, block, points)
    pl.semaphore_wait(barrier, n - 1 + len(others))
    exchange([(0, sent, got)])
    arrived = got[...].reshape(n, planes, planes, points)
    for x in range(planes):
        column = arrived[:, x].reshape(points, points)
        weighted = coulomb[x] * full_dot(basis[...], column)
        back_h[:, x * planes : (x + 1) * planes] = table_left(basis_2, weighted).reshape(n, planes, points)
        back_y[:, x * planes : (x + 1) * planes] = table_left(slope_2, column).reshape(n, planes, points)
    exchange([(1, back_h, got_h), (2, back_y, got_y)])

    first = band * share if share < planes else 0
    for i in range(share):
        y = first + i
        both = jnp.concatenate(
            [got_h[pl.ds(y, points, stride=planes), :], got_y[pl.ds(y, points, stride=planes), :]], 1
        )
        both = table_left(basis_2, both)
        both = table_right(jnp.concatenate([both[:, :points], both[:, points:]], 0), basis_2)
        hartree = both[:points]
        change_y = both[points:] * (1.0 / (points * points))
        varying = density[y] - 2.275
        change_x = table_left(slope_2, varying)
        change_z = table_right(varying, slope_t2)
        gradient = jnp.sqrt(change_x * change_x + change_y * change_y + change_z * change_z)
        root = cube[y]
        reduced = gradient / (reduced_scale * density[y] * root)
        bounded = reduced / (1.0 + reduced)

        def unit(k, total):
            return total + mlp_out[k] * jnp.tanh(mlp_in[0, k] * root + mlp_in[1, k] * bounded + mlp_in[2, k])

        enhance = lax.fori_loop(0, hidden, unit, jnp.ones_like(root), unroll=4)
        out[y] = external[y] + hartree - exchange_scale * root * enhance

    def shared(i, whose):
        part = out.at[pl.ds(whose * share, share)]
        return pltpu.make_async_remote_copy(
            src_ref=part,
            dst_ref=part,
            send_sem=share_sem.at[0, i - 1],
            recv_sem=share_sem.at[1, i - 1],
            device_id={"band": lax.rem(band + i, peers), "grid": me},
            device_id_type=MESH,
        )

    for i in others:
        shared(i, band).start()
    for i in others:
        shared(i, band).wait_send()
        shared(i, lax.rem(band + peers - i, peers)).wait_recv()


def body(coefficients, potential, external, core_density, rotations, mlp_in, mlp_out):
    points = potential.shape[1]
    planes = coefficients.shape[2]
    n, peers = lax.axis_size("grid"), lax.axis_size("band")
    offset = lax.axis_index("grid") * planes
    coulomb = reciprocal_tables(points, offset, planes) * (1.0 / points**3)
    current, density = update_bands(coefficients, potential, core_density, rotations)

    cell = np.arange(points)
    angle = 2.0 * np.pi * ((cell[:, None] * cell[None, :]) % points) / points
    freq = np.where(2 * cell < points, cell, cell - points)
    slope = gradient_scale * np.where(2 * freq == -points, 0, freq) / points
    back = (np.exp(1j * angle) * slope[None, :] * 1j) @ np.exp(-1j * angle) / points
    slope_table = np.ascontiguousarray(back.real).astype(np.float32)
    basis = (np.cos(angle) + np.sin(angle)).astype(np.float32)
    vmem = pl.BlockSpec(memory_space=pltpu.VMEM)
    smem = pl.BlockSpec(memory_space=pltpu.SMEM)
    block = planes * planes
    new_potential = pl.pallas_call(
        functools.partial(field_kernel, n, peers, points, mlp_out.shape[0]),
        out_shape=jax.ShapeDtypeStruct((planes, points, points), F32),
        in_specs=[vmem] * 8 + [smem, smem],
        out_specs=vmem,
        scratch_shapes=[
            pltpu.VMEM((n * block, points), F32),
            pltpu.VMEM((n, block, points), F32),
            pltpu.VMEM((n * block, points), F32),
            pltpu.VMEM((n, block, points), F32),
            pltpu.VMEM((n, block, points), F32),
            pltpu.VMEM((n * block, points), F32),
            pltpu.VMEM((n * block, points), F32),
            pltpu.SemaphoreType.DMA((3, n)),
            pltpu.SemaphoreType.DMA((3, n)),
            pltpu.SemaphoreType.DMA((2, max(peers - 1, 1))),
        ],
        compiler_params=pltpu.CompilerParams(
            collective_id=1, has_side_effects=True, vmem_limit_bytes=40 * 2**20
        ),
    )(
        density, jnp.cbrt(density), external, coulomb, basis,
        halves(basis), halves(slope_table), halves(slope_table.T), mlp_in, mlp_out,
    )
    return (current, new_potential)


def solution(mesh):
    in_specs = (
        P("band", None, "grid", None, None),
        P("grid", None, None),
        P("grid", None, None),
        P("grid", None, None),
        P(None, "band", None),
        P(),
        P(),
    )
    out_specs = (P("band", None, "grid", None, None), P("grid", None, None))
    return jax.shard_map(body, mesh=mesh, in_specs=in_specs, out_specs=out_specs, check_vma=False)
```
